32 devices in a mesh: blk: 4 (over x, core), uly: 8 (over z, y).
Axes of the slice: x: 2, y: 2, z: 4, core: 2. Of those that a mesh axis runs over, the one named last changes fastest.
Arguments:
- query_rows: bfloat16 [4096, 512], P(('blk', 'uly')), may hold values from -6 to 6
- key_rows: bfloat16 [4096, 512], P(('blk', 'uly')), may hold values from -6 to 6
- value_rows: bfloat16 [4096, 512], P(('blk', 'uly')), may hold values from -6 to 6
- out_grad: bfloat16 [4096, 512], P(('blk', 'uly')), may hold values from -6 to 6
- block_lists: int32 [64, 8], P('blk'), may hold values from 0 to 63, as said below
- block_counts: int32 [64], P('blk'), may hold values from 1 to 8
Outputs:
- attended: bfloat16 [4096, 512], P(('blk', 'uly'))
- query_gradient: bfloat16 [4096, 512], P(('blk', 'uly'))
- key_grad: bfloat16 [4096, 512], P(('blk', 'uly'))
- value_grad: bfloat16 [4096, 512], P(('blk', 'uly'))
The draws below stay inside these ranges and needn't reach their ends.
Inputs may be any that keep to these rules, and one draw needn't show every extreme that they name: `block_lists`: row b lists key blocks of query block b: entry 0 is b, entries 1 to block_counts[b] - 1 are distinct blocks other than b, and the remaining entries equal b.
All inputs are finite; a program needn't handle non-finite values.
Results may differ from the reference program's by a relative error of at most 0.02.
Values may be sent and summed in bfloat16 or wider, within the bound.
A program may use at most 128 MiB of HBM per device.

```python
import math
import jax
import jax.numpy as jnp
from jax import lax

HDIM = 64
BLK = 64
KSEL = 8
HEADS = 8
WIDTH = 512
TOKENS = 4096
NQB = 64


def routing_pair(key):
    base = jax.random.fold_in(key, 11)
    count_key, list_key = jax.random.split(base)
    counts = jax.random.randint(count_key, (NQB,), 1, KSEL + 1)
    counts = counts.at[0].set(KSEL).at[1].set(1)
    own = jnp.arange(NQB)
    logit_matrix = jax.random.randint(list_key, (NQB, NQB), 0, 4096) * NQB + own[None, :]
    logit_matrix = jnp.where(own[:, None] == own[None, :], 4096 * NQB + NQB, logit_matrix)
    chosen = lax.top_k(logit_matrix, KSEL)[1]
    slot_ids = jnp.arange(KSEL)[None, :]
    lists = jnp.where(slot_ids < counts[:, None], chosen, own[:, None])
    return (lists.astype(jnp.int32), counts.astype(jnp.int32))


def draw_block_lists(key, part):
    return routing_pair(key)[0]


def draw_block_counts(key, part):
    return routing_pair(key)[1]


def query_key_pair(key):
    base = jax.random.fold_in(key, 23)
    query_key, key_key = jax.random.split(base, 2)
    shape = (TOKENS, HEADS, HDIM)
    query_matrix = jnp.clip(jax.random.normal(query_key, shape, jnp.float32), -6.0, 6.0)
    keys_drawn = jnp.clip(jax.random.normal(key_key, shape, jnp.float32), -6.0, 6.0)
    return (query_matrix.reshape(TOKENS, WIDTH), keys_drawn.reshape(TOKENS, WIDTH))


def draw_query_rows(key, part):
    return query_key_pair(key)[0].astype(jnp.bfloat16)


def draw_key_rows(key, part):
    return query_key_pair(key)[1].astype(jnp.bfloat16)


def steps_of(rng, shape, cuts, low, largest):
    def one(dim, shards_of):
        heights = jax.random.uniform(jax.random.fold_in(jax.random.fold_in(rng, 6), dim), (shards_of,), jnp.float32, low / len(cuts), largest / len(cuts))
        return jnp.repeat(jnp.exp(heights), shape[dim] // shards_of).reshape((-1,) + (1,) * (len(shape) - dim - 1))

    loudness = one(*cuts[0])
    for cut in cuts[1:]:
        loudness = loudness * one(*cut)
    return loudness


def gaussian(key, shape, deviation, bound, shards=(), kind=jnp.bfloat16):
    loudness = steps_of(key, shape, shards, -0.22, 0.18) if shards else 1.0
    result = jax.random.normal(key, shape, jnp.float32) * deviation * loudness
    return jnp.minimum(jnp.maximum(result, -bound), bound).astype(kind)


def setup_inputs(seed: int = 0) -> dict:
    key_of = jax.random.split(jax.random.key(seed), 7)
    return {
        "query_rows": draw_query_rows(jax.random.fold_in(key_of[6], 71), 0),
        "key_rows": draw_key_rows(jax.random.fold_in(key_of[6], 71), 0),
        "value_rows": gaussian(key_of[2], (TOKENS, WIDTH), 1.0, 6.0, ((0, 32),)),
        "out_grad": gaussian(key_of[3], (TOKENS, WIDTH), 1.0, 6.0, ((0, 32),)),
        "block_lists": draw_block_lists(jax.random.fold_in(key_of[6], 71), 0),
        "block_counts": draw_block_counts(jax.random.fold_in(key_of[6], 71), 0),
    }


def head_pass(operands, block_lists, block_counts):
    query_head, key_head, value_head, grad_head = operands
    softmax_scale = 1.0 / math.sqrt(HDIM)
    query_matrix = query_head.reshape(NQB, BLK, HDIM).astype(jnp.float32)
    gradient_tuple = grad_head.reshape(NQB, BLK, HDIM).astype(jnp.float32)
    gathered_key_blocks = key_head.reshape(NQB, BLK, HDIM)[block_lists].astype(jnp.float32)
    gathered_value_blocks = value_head.reshape(NQB, BLK, HDIM)[block_lists].astype(jnp.float32)
    usable = (jnp.arange(KSEL)[None, :] < block_counts[:, None])[:, None, :, None]
    logit_matrix = jnp.einsum('yxe,yale->yxal', query_matrix, gathered_key_blocks) * softmax_scale
    row_max = lax.optimization_barrier(jnp.max(jnp.where(usable, logit_matrix, -1e+30), axis=(2, 3), keepdims=True))
    weights = jnp.where(usable, jnp.exp(logit_matrix - row_max), 0.0)
    probability = weights / lax.optimization_barrier(jnp.sum(weights, axis=(2, 3), keepdims=True))
    reduced_precision = lax.optimization_barrier(probability.astype(jnp.bfloat16)).astype(jnp.float32)
    attended = jnp.einsum('mexl,mxlf->mef', reduced_precision, gathered_value_blocks).astype(jnp.bfloat16)
    delta = lax.optimization_barrier(jnp.sum(gradient_tuple * attended.astype(jnp.float32), axis=-1))[:, :, None, None]
    probability_gradient = jnp.einsum('yxe,yale->yxal', gradient_tuple, gathered_value_blocks)
    score_gradient = lax.optimization_barrier((probability * (probability_gradient - delta)).astype(jnp.bfloat16)).astype(jnp.float32)
    query_gradient = (jnp.einsum('mexl,mxlf->mef', score_gradient, gathered_key_blocks) * softmax_scale).astype(jnp.bfloat16)
    key_contribution = jnp.einsum('nmpc,nmu->npcu', score_gradient, query_matrix) * softmax_scale
    value_contribution = jnp.einsum('nmpc,nmu->npcu', reduced_precision, gradient_tuple)
    key_grad = jnp.zeros((NQB, BLK, HDIM), jnp.float32).at[block_lists].add(key_contribution).astype(jnp.bfloat16)
    value_grad = jnp.zeros((NQB, BLK, HDIM), jnp.float32).at[block_lists].add(value_contribution).astype(jnp.bfloat16)
    return (attended.reshape(TOKENS, HDIM), query_gradient.reshape(TOKENS, HDIM), key_grad.reshape(TOKENS, HDIM), value_grad.reshape(TOKENS, HDIM))

def reference(query_rows, key_rows, value_rows, out_grad, block_lists, block_counts):

    def by_head(array):
        return array.reshape(TOKENS, HEADS, HDIM).transpose(1, 0, 2)

    def one_head(operands):
        return head_pass(operands, block_lists, block_counts)
    results = lax.map(one_head, (by_head(query_rows), by_head(key_rows), by_head(value_rows), by_head(out_grad)))

    def back(array):
        return array.transpose(1, 0, 2).reshape(TOKENS, WIDTH)
    return (back(results[0]), back(results[1]), back(results[2]), back(results[3]))
```

```python
import functools
import math

import jax
import jax.numpy as jnp
from jax import lax
from jax.experimental import pallas as pl
from jax.experimental.pallas import tpu as pltpu
from jax.sharding import PartitionSpec as P

HDIM = 64
BLK = 64
KSEL = 8
PAIR = 2 * HDIM
SCALE = 1.0 / math.sqrt(HDIM)
VMEM_BYTES = 56 * 1024 * 1024


def dot(a, b, dims):
    return lax.dot_general(a, b, (dims, ((), ())), preferred_element_type=jnp.float32)


def attention_kernel(group, lists, counts, qd_ref, kv_ref, od_ref, dkv_ref, acc):
    local_blocks = qd_ref.shape[0] // BLK
    acc[...] = jnp.zeros_like(acc)
    first = lax.broadcasted_iota(jnp.int32, (BLK, PAIR), 1) < HDIM
    column = lax.broadcasted_iota(jnp.int32, (BLK, KSEL * BLK), 1)

    def one_block(b):
        rows = pl.ds(pl.multiple_of(b * BLK, BLK), BLK)
        picks = [pl.ds(pl.multiple_of(lists[b, j] * BLK, BLK), BLK) for j in range(KSEL)]
        qd = qd_ref[rows, :]
        zero = jnp.zeros_like(qd)
        diag = jnp.concatenate([jnp.where(first, qd, zero), jnp.where(first, zero, qd)], axis=0)
        kv = jnp.concatenate([kv_ref[pick, :] for pick in picks], axis=0)
        both = dot(diag, kv, ((1,), (1,)))
        scores = jnp.where(column < counts[b] * BLK, both[:BLK] * SCALE, -1e30)
        weights = jnp.exp(scores - jnp.max(scores, axis=1, keepdims=True))
        prob = weights * (1.0 / jnp.sum(weights, axis=1, keepdims=True))
        rounded = prob.astype(jnp.bfloat16)
        out = dot(rounded, kv, ((1,), (0,))).astype(jnp.bfloat16).astype(jnp.float32)
        delta = jnp.sum(jnp.where(first, 0.0, qd.astype(jnp.float32) * out), axis=1, keepdims=True)
        grad_score = (prob * (both[BLK:] - delta)).astype(jnp.bfloat16)
        dq = dot(grad_score, kv, ((1,), (0,))) * SCALE
        od_ref[rows, :] = jnp.where(first, dq, out).astype(jnp.bfloat16)
        terms = dot(jnp.concatenate([grad_score, rounded], axis=0), diag, ((0,), (0,)))
        return picks, terms

    def turn(g, carry):
        done = [one_block(g * group + i) for i in range(group)]
        for picks, terms in done:
            for j, pick in enumerate(picks):
                acc[pick, :] += terms[j * BLK : (j + 1) * BLK]
        return carry

    lax.fori_loop(0, local_blocks // group, turn, 0)
    lane = lax.broadcasted_iota(jnp.int32, (1, PAIR), 1)
    dkv_ref[...] = (acc[...] * jnp.where(lane < HDIM, SCALE, 1.0)).astype(dkv_ref.dtype)


def attention(block_lists, block_counts, qd, kv):
    heads_here, seg_rows, _ = qd.shape
    all_rows = kv.shape[1]

    def spec(rows):
        kind = {"pipeline_mode": pl.Buffered(1)} if heads_here > 1 else {}
        return pl.BlockSpec((None, rows, PAIR), lambda h, *_: (h, 0, 0), **kind)

    return pl.pallas_call(
        functools.partial(attention_kernel, math.gcd(2, seg_rows // BLK)),
        out_shape=(
            jax.ShapeDtypeStruct((heads_here, seg_rows, PAIR), jnp.bfloat16),
            jax.ShapeDtypeStruct((heads_here, all_rows, PAIR), jnp.bfloat16),
        ),
        grid_spec=pltpu.PrefetchScalarGridSpec(
            num_scalar_prefetch=2,
            grid=(heads_here,),
            in_specs=[spec(seg_rows), spec(all_rows)],
            out_specs=[spec(seg_rows), spec(all_rows)],
            scratch_shapes=[pltpu.VMEM((all_rows, PAIR), jnp.float32)],
        ),
        compiler_params=pltpu.CompilerParams(vmem_limit_bytes=VMEM_BYTES),
        name="attention",
    )(block_lists, block_counts, qd, kv)


def on_device(query_rows, key_rows, value_rows, out_grad, block_lists, block_counts):
    rows, width = query_rows.shape
    heads = width // HDIM

    def by_head(array):
        return array.reshape(rows, heads, HDIM)

    packed = jnp.concatenate([by_head(a) for a in (query_rows, out_grad, key_rows, value_rows)], axis=2)
    packed = packed.transpose(1, 0, 2)
    seg = lax.all_to_all(packed, "uly", split_axis=0, concat_axis=1, tiled=True)
    qd = seg[..., :PAIR]
    kv = lax.all_gather(seg[..., PAIR:], "blk", axis=1, tiled=True)
    od, dkv = attention(block_lists, block_counts, qd, kv)
    dkv = lax.psum_scatter(dkv.astype(jnp.float32), "blk", scatter_dimension=1, tiled=True)
    both = jnp.concatenate([od, dkv.astype(jnp.bfloat16)], axis=2)
    back = lax.all_to_all(both, "uly", split_axis=1, concat_axis=0, tiled=True)
    back = back.transpose(1, 0, 2).reshape(rows, heads, 4, HDIM)
    dq, out, dk, dv = (back[:, :, i].reshape(rows, width) for i in range(4))
    return out, dq, dk, dv


def solution(mesh):
    tokens = P(("blk", "uly"), None)
    return jax.shard_map(
        on_device,
        mesh=mesh,
        in_specs=(tokens, tokens, tokens, tokens, P("blk", None), P("blk")),
        out_specs=(tokens, tokens, tokens, tokens),
        check_vma=False,
    )
```

```python
import functools
import math

import jax
import jax.numpy as jnp
from jax import lax
from jax.experimental import pallas as pl
from jax.experimental.pallas import tpu as pltpu
from jax.sharding import PartitionSpec as P

HDIM = 64
BLK = 64
KSEL = 8
PAIR = 2 * HDIM
SCALE = 1.0 / math.sqrt(HDIM)
VMEM_BYTES = 56 * 1024 * 1024


def dot(a, b, dims):
    return lax.dot_general(a, b, (dims, ((), ())), preferred_element_type=jnp.float32)


def attention_kernel(group, lists, counts, qd_ref, kv_ref, od_ref, dkv_ref, acc):
    local_blocks = qd_ref.shape[0] // BLK
    acc[...] = jnp.zeros_like(acc)
    first = lax.broadcasted_iota(jnp.int32, (BLK, PAIR), 1) < HDIM
    column = lax.broadcasted_iota(jnp.int32, (BLK, KSEL * BLK), 1)

    def one_block(b):
        rows = pl.ds(pl.multiple_of(b * BLK, BLK), BLK)
        picks = [pl.ds(pl.multiple_of(lists[b, j] * BLK, BLK), BLK) for j in range(KSEL)]
        qd = qd_ref[rows, :]
        zero = jnp.zeros_like(qd)
        diag = jnp.concatenate([jnp.where(first, qd, zero), jnp.where(first, zero, qd)], axis=0)
        kv = jnp.concatenate([kv_ref[pick, :] for pick in picks], axis=0)
        both = dot(diag, kv, ((1,), (1,)))
        scores = jnp.where(column < counts[b] * BLK, both[:BLK] * SCALE, -1e30)
        weights = jnp.exp(scores - jnp.max(scores, axis=1, keepdims=True))
        prob = weights * (1.0 / jnp.sum(weights, axis=1, keepdims=True))
        rounded = prob.astype(jnp.bfloat16)
        out = dot(rounded, kv, ((1,), (0,))).astype(jnp.bfloat16).astype(jnp.float32)
        delta = jnp.sum(jnp.where(first, 0.0, qd.astype(jnp.float32) * out), axis=1, keepdims=True)
        grad_score = (prob * (both[BLK:] - delta)).astype(jnp.bfloat16)
        dq = dot(grad_score, kv, ((1,), (0,))) * SCALE
        od_ref[rows, :] = jnp.where(first, dq, out).astype(jnp.bfloat16)
        terms = dot(jnp.concatenate([grad_score, rounded], axis=0), diag, ((0,), (0,)))
        return picks, terms

    def turn(g, carry):
        done = [one_block(g * group + i) for i in range(group)]
        for picks, terms in done:
            for j, pick in enumerate(picks):
                acc[pick, :] += terms[j * BLK : (j + 1) * BLK]
        return carry

    lax.fori_loop(0, local_blocks // group, turn, 0)
    lane = lax.broadcasted_iota(jnp.int32, (1, PAIR), 1)
    dkv_ref[...] = (acc[...] * jnp.where(lane < HDIM, SCALE, 1.0)).astype(dkv_ref.dtype)


def attention(block_lists, block_counts, qd, kv):
    heads_here, seg_rows, _ = qd.shape
    all_rows = kv.shape[1]

    def spec(rows):
        kind = {"pipeline_mode": pl.Buffered(1)} if heads_here > 1 else {}
        return pl.BlockSpec((None, rows, PAIR), lambda h, *_: (h, 0, 0), **kind)

    return pl.pallas_call(
        functools.partial(attention_kernel, math.gcd(2, seg_rows // BLK)),
        out_shape=(
            jax.ShapeDtypeStruct((heads_here, seg_rows, PAIR), jnp.bfloat16),
            jax.ShapeDtypeStruct((heads_here, all_rows, PAIR), jnp.bfloat16),
        ),
        grid_spec=pltpu.PrefetchScalarGridSpec(
            num_scalar_prefetch=2,
            grid=(heads_here,),
            in_specs=[spec(seg_rows), spec(all_rows)],
            out_specs=[spec(seg_rows), spec(all_rows)],
            scratch_shapes=[pltpu.VMEM((all_rows, PAIR), jnp.float32)],
        ),
        compiler_params=pltpu.CompilerParams(vmem_limit_bytes=VMEM_BYTES),
        name="attention",
    )(block_lists, block_counts, qd, kv)


MESH = pl.DeviceIdType.MESH


def places():
    seg, lane = lax.axis_index("blk"), lax.axis_index("uly")
    core = lax.rem(seg, 2)
    return seg, lane, seg + 1 - 2 * core, lax.rem(seg + 2, 4)


def remote(src, dst, send, recv, device):
    return pltpu.make_async_remote_copy(
        src_ref=src, dst_ref=dst, send_sem=send, recv_sem=recv, device_id=device, device_id_type=MESH
    )


def greet(lanes):
    seg, lane, other, across = places()
    barrier = pltpu.get_barrier_semaphore()

    def one(i, carry):
        device = (seg, lax.rem(lane + i, lanes))
        pl.semaphore_signal(barrier, inc=1, device_id=device, device_id_type=MESH)
        return carry

    lax.fori_loop(1, lanes, one, 0)
    for near in (other, across):
        pl.semaphore_signal(barrier, inc=1, device_id=(near, lane), device_id_type=MESH)
    return barrier


def loop(start, stop, body):
    lax.fori_loop(start, stop, lambda i, carry: (body(i), carry)[1], 0)


def join(left, right):
    return jnp.concatenate([left, right], axis=1)


def gather_kernel(
    lanes, q_ref, k_ref, v_ref, g_ref, qd, kv, qd_out, kv_out, qd_s, qd_r, kv_s, kv_r, x_s, x_r, c_s, c_r
):
    seg, lane, other, across = places()
    heads_here = qd.shape[1]
    barrier = greet(lanes)

    def pack(left, right, to):
        for h in range(lanes * heads_here):
            columns = slice(h * HDIM, (h + 1) * HDIM)
            to[h // heads_here, h % heads_here] = join(left[:, columns], right[:, columns])

    pack(k_ref, v_ref, kv_out)
    pl.semaphore_wait(barrier, lanes + 1)

    def kv_copy(i, target, source):
        return remote(kv_out.at[target], kv.at[seg, source], kv_s.at[i], kv_r.at[i], (seg, target))

    def qd_copy(i, target, source):
        return remote(qd_out.at[target], qd.at[source], qd_s.at[i], qd_r.at[i], (seg, target))

    def x_copy(i, source, whose):
        return remote(kv.at[whose, source], kv.at[whose, source], x_s.at[i], x_r.at[i], (across, lane))

    def c_copy(n, i, source, whose):
        block = kv.at[whose, source]
        return remote(block, block, c_s.at[n, i], c_r.at[n, i], (other, lane))

    def ahead(i):
        return lax.rem(lane + i, lanes)

    def behind(i):
        return lax.rem(lane + lanes - i, lanes)

    loop(1, lanes, lambda i: kv_copy(i, ahead(i), lane).start())
    kv[seg, lane] = kv_out[lane]
    x_copy(0, lane, seg).start()
    c_copy(0, 0, lane, seg).start()
    pack(q_ref, g_ref, qd_out)
    loop(1, lanes, lambda i: qd_copy(i, ahead(i), lane).start())
    qd[lane] = qd_out[lane]

    def relay(i):
        x_copy(i, behind(i), across).wait_recv()
        c_copy(1, i, behind(i), across).start()

    def arrive(i):
        kv_copy(i, lane, behind(i)).wait_recv()
        x_copy(i, behind(i), seg).start()
        c_copy(0, i, behind(i), seg).start()
        relay(i - 1)

    loop(1, lanes, arrive)
    relay(lanes - 1)

    def finish(i):
        c_copy(0, i, behind(i), other).wait_recv()
        c_copy(1, i, behind(i), lax.rem(other + 2, 4)).wait_recv()
        x_copy(i, behind(i), seg).wait_send()
        c_copy(0, i, behind(i), seg).wait_send()
        c_copy(1, i, behind(i), across).wait_send()

    loop(0, lanes, finish)

    def finish_lanes(i):
        qd_copy(i, lane, behind(i)).wait_recv()
        qd_copy(i, ahead(i), lane).wait_send()
        kv_copy(i, ahead(i), lane).wait_send()

    loop(1, lanes, finish_lanes)


def return_kernel(
    lanes, od, dkv, out_ref, dq_ref, dk_ref, dv_ref,
    od_in, core_in, x_out, x_in, end_out, end_in,
    od_s, od_r, c_s, c_r, x_s, x_r, e_s, e_r,
):
    seg, lane, other, across = places()
    heads_here = od.shape[1]
    barrier = greet(lanes)

    def ahead(i):
        return lax.rem(lane + i, lanes)

    def behind(i):
        return lax.rem(lane + lanes - i, lanes)

    def od_copy(i, target, source):
        return remote(od.at[target], od_in.at[source], od_s.at[i], od_r.at[i], (seg, target))

    def end_copy(i, target, source):
        return remote(end_out.at[target], end_in.at[source], e_s.at[i], e_r.at[i], (seg, target))

    def c_copy(n, i, whose):
        return remote(dkv.at[whose, ahead(i)], core_in.at[n, ahead(i)], c_s.at[n, i], c_r.at[n, i], (other, lane))

    def x_copy(i):
        return remote(x_out.at[ahead(i)], x_in.at[ahead(i)], x_s.at[i], x_r.at[i], (across, lane))

    def send(i):
        c_copy(1, i, lax.rem(other + 2, 4)).start()
        c_copy(0, i, other).start()

    def wide(block):
        return block.astype(jnp.float32)

    def reduce_core(i):
        c_copy(1, i, other).wait_recv()
        to = ahead(i)
        x_out[to] = (wide(dkv[across, to]) + wide(core_in[1, to])).astype(jnp.bfloat16)
        x_copy(i).start()

    def total(i):
        c_copy(0, i, other).wait_recv()
        x_copy(i).wait_recv()
        to = ahead(i)
        return (wide(dkv[seg, to]) + wide(core_in[0, to]) + wide(x_in[to])).astype(jnp.bfloat16)

    def reduce_chip(i):
        end_out[ahead(i)] = total(i)
        end_copy(i, ahead(i), lane).start()

    lag = min(2, lanes - 1)
    pl.semaphore_wait(barrier, lanes + 1)
    loop(1, lanes + 1, send)
    loop(1, lanes, lambda i: od_copy(i, ahead(i), lane).start())
    od_in[lane] = od[lane]
    loop(1, lag + 1, reduce_core)

    def both(i):
        reduce_core(i)
        reduce_chip(i - lag)

    loop(lag + 1, lanes + 1, both)
    loop(lanes + 1 - lag, lanes, reduce_chip)
    end_in[lane] = total(lanes)

    def unpack(block, left, right):
        for h in range(0, lanes * heads_here, 2):
            a, b = (block[g // heads_here, g % heads_here] for g in (h, h + 1))
            columns = slice(h * HDIM, (h + 2) * HDIM)
            left[:, columns] = join(a[:, :HDIM], b[:, :HDIM])
            right[:, columns] = join(a[:, HDIM:], b[:, HDIM:])

    loop(1, lanes, lambda i: od_copy(i, lane, behind(i)).wait_recv())
    unpack(od_in, dq_ref, out_ref)
    loop(1, lanes, lambda i: end_copy(i, lane, behind(i)).wait_recv())
    unpack(end_in, dk_ref, dv_ref)

    def finish(i):
        c_copy(0, i, other).wait_send()
        c_copy(1, i, other).wait_send()
        x_copy(i).wait_send()

    loop(1, lanes + 1, finish)

    def finish_lanes(i):
        od_copy(i, ahead(i), lane).wait_send()
        end_copy(i, ahead(i), lane).wait_send()

    loop(1, lanes, finish_lanes)


def comm_params(number):
    return pltpu.CompilerParams(
        collective_id=number, has_side_effects=True, vmem_limit_bytes=VMEM_BYTES
    )


def on_device(lanes, query_rows, key_rows, value_rows, out_grad, block_lists, block_counts):
    rows, width = query_rows.shape
    heads_here = width // HDIM // lanes
    segs = 4
    block = (heads_here, rows, PAIR)
    vmem = pl.BlockSpec(memory_space=pltpu.VMEM)
    dma = pltpu.SemaphoreType.DMA
    half = jnp.bfloat16

    qd, kv = pl.pallas_call(
        functools.partial(gather_kernel, lanes),
        out_shape=(
            jax.ShapeDtypeStruct((lanes, *block), half),
            jax.ShapeDtypeStruct((segs, lanes, *block), half),
        ),
        in_specs=[vmem] * 4,
        out_specs=(vmem, vmem),
        scratch_shapes=[pltpu.VMEM((lanes, *block), half)] * 2
        + [dma((lanes,))] * 6
        + [dma((2, lanes))] * 2,
        compiler_params=comm_params(0),
        name="gather",
    )(query_rows, key_rows, value_rows, out_grad)

    qd = qd.transpose(1, 0, 2, 3).reshape(heads_here, lanes * rows, PAIR)
    kv = kv.transpose(2, 0, 1, 3, 4).reshape(heads_here, segs * lanes * rows, PAIR)
    od, dkv = attention(block_lists, block_counts, qd, kv)
    od = od.reshape(heads_here, lanes, rows, PAIR).transpose(1, 0, 2, 3)
    dkv = dkv.reshape(heads_here, segs, lanes, rows, PAIR).transpose(1, 2, 0, 3, 4)

    return tuple(
        pl.pallas_call(
            functools.partial(return_kernel, lanes),
            out_shape=[jax.ShapeDtypeStruct((rows, width), half)] * 4,
            in_specs=[vmem] * 2,
            out_specs=[vmem] * 4,
            scratch_shapes=[
                pltpu.VMEM((lanes, *block), half),
                pltpu.VMEM((2, lanes, *block), half),
            ]
            + [pltpu.VMEM((lanes, *block), half)] * 4
            + [dma((lanes + 1,))] * 2
            + [dma((2, lanes + 1))] * 2
            + [dma((lanes + 1,))] * 4,
            compiler_params=comm_params(1),
            name="scatter",
        )(od, dkv)
    )


def solution(mesh):
    tokens = P(("blk", "uly"), None)
    return jax.shard_map(
        functools.partial(on_device, mesh.shape["uly"]),
        mesh=mesh,
        in_specs=(tokens, tokens, tokens, tokens, P("blk", None), P("blk")),
        out_specs=(tokens, tokens, tokens, tokens),
        check_vma=False,
    )
```

```python
import functools
import math

import jax
import jax.numpy as jnp
from jax import lax
from jax.experimental import pallas as pl
from jax.experimental.pallas import tpu as pltpu
from jax.sharding import PartitionSpec as P

HDIM = 64
BLK = 64
KSEL = 8
PAIR = 2 * HDIM
SCALE = 1.0 / math.sqrt(HDIM)
GROUP = 8
MIB = 1024 * 1024


def dot(a, b, dims):
    return lax.dot_general(a, b, (dims, ((), ())), preferred_element_type=jnp.float32)


def attention_kernel(group, lists_hbm, counts_hbm, qd, kv, od, dkv, lists, counts, acc, sems):
    loads = (
        pltpu.make_async_copy(lists_hbm, lists, sems.at[0]),
        pltpu.make_async_copy(counts_hbm, counts, sems.at[1]),
    )
    for load in loads:
        load.start()
    for h in range(qd.shape[0]):
        acc[...] = jnp.zeros_like(acc)
        if h == 0:
            for load in loads:
                load.wait()
        attend_head(group, lists, counts, qd.at[h], kv.at[h], od.at[h], acc)
        dkv[h] = acc[...].astype(dkv.dtype)


def attend_head(group, lists, counts, qd_ref, kv_ref, od_ref, acc):
    local_blocks = qd_ref.shape[0] // BLK
    lane = lax.broadcasted_iota(jnp.int32, (BLK, PAIR), 1)
    first = lane < HDIM
    column = lax.broadcasted_iota(jnp.int32, (BLK, KSEL * BLK), 1)

    def one_block(b):
        rows = pl.ds(pl.multiple_of(b * BLK, BLK), BLK)
        picks = [pl.ds(pl.multiple_of(lists[j, b] * BLK, BLK), BLK) for j in range(KSEL)]
        qd = qd_ref[rows, :]
        zero = jnp.zeros_like(qd)
        diag = jnp.concatenate([jnp.where(first, qd * SCALE, zero), jnp.where(first, zero, qd)], axis=0)
        kv = jnp.concatenate([kv_ref[pick, :] for pick in picks], axis=0)
        both = dot(diag, kv, ((1,), (1,)))
        scores = jnp.where(column < counts[b] * BLK, both[:BLK], -1e30)
        weights = jnp.exp(scores - jnp.max(scores, axis=1, keepdims=True))
        prob = weights * (1.0 / jnp.sum(weights, axis=1, keepdims=True))
        rounded = prob.astype(jnp.bfloat16)
        delta = jnp.sum(rounded.astype(jnp.float32) * both[BLK:], axis=1, keepdims=True)
        grad_score = (prob * (both[BLK:] - delta)).astype(jnp.bfloat16)
        stacked = jnp.concatenate([grad_score, rounded], axis=0)
        rows_out = dot(stacked, kv, ((1,), (0,)))
        od_ref[rows, :] = jnp.where(first, rows_out[:BLK] * SCALE, rows_out[BLK:]).astype(jnp.bfloat16)
        terms = dot(stacked, diag, ((0,), (0,)))
        return picks, terms

    def turn(g, carry):
        done = [one_block(g * group + i) for i in range(group)]
        for picks, terms in done:
            for j, pick in enumerate(picks):
                acc[pick, :] += terms[j * BLK : (j + 1) * BLK]
        return carry

    lax.fori_loop(0, local_blocks // group, turn, 0)

def attention(block_lists, block_counts, qd, kv):
    heads_here, seg_rows, _ = qd.shape
    all_rows = kv.shape[1]
    vmem = pl.BlockSpec(memory_space=pltpu.VMEM)
    hbm = pl.BlockSpec(memory_space=pltpu.HBM)
    lists = block_lists.T
    limit = 6 * MIB + 4 * all_rows * PAIR + 4 * heads_here * (all_rows + seg_rows) * PAIR
    return pl.pallas_call(
        functools.partial(attention_kernel, math.gcd(GROUP, seg_rows // BLK)),
        out_shape=(
            jax.ShapeDtypeStruct(qd.shape, jnp.bfloat16),
            jax.ShapeDtypeStruct(kv.shape, jnp.bfloat16),
        ),
        in_specs=[hbm, hbm, vmem, vmem],
        out_specs=(vmem, vmem),
        scratch_shapes=[
            pltpu.SMEM(lists.shape, jnp.int32),
            pltpu.SMEM(block_counts.shape, jnp.int32),
            pltpu.VMEM((all_rows, PAIR), jnp.float32),
            pltpu.SemaphoreType.DMA((2,)),
        ],
        compiler_params=pltpu.CompilerParams(vmem_limit_bytes=limit),
        name="attention",
    )(
        pltpu.with_memory_space_constraint(lists, pltpu.HBM),
        pltpu.with_memory_space_constraint(block_counts, pltpu.HBM),
        qd,
        kv,
    )


MESH = pl.DeviceIdType.MESH


def places():
    seg, lane = lax.axis_index("blk"), lax.axis_index("uly")
    core = lax.rem(seg, 2)
    return seg, lane, seg + 1 - 2 * core, lax.rem(seg + 2, 4)


def remote(src, dst, send, recv, device):
    return pltpu.make_async_remote_copy(
        src_ref=src, dst_ref=dst, send_sem=send, recv_sem=recv, device_id=device, device_id_type=MESH
    )


def greet(lanes):
    seg, lane, other, across = places()
    barrier = pltpu.get_barrier_semaphore()

    def one(i, carry):
        device = (seg, lax.rem(lane + i, lanes))
        pl.semaphore_signal(barrier, inc=1, device_id=device, device_id_type=MESH)
        return carry

    lax.fori_loop(1, lanes, one, 0)
    for near in (other, across):
        pl.semaphore_signal(barrier, inc=1, device_id=(near, lane), device_id_type=MESH)
    return barrier


def loop(start, stop, body):
    lax.fori_loop(start, stop, lambda i, carry: (body(i), carry)[1], 0)


def join(left, right):
    return jnp.concatenate([left, right], axis=1)


def gather_kernel(
    lanes, q_hbm, k_hbm, v_hbm, g_hbm, qd, kv,
    k_ref, v_ref, q_ref, g_ref, qd_out, kv_out, in_s, qd_s, qd_r, kv_s, kv_r, x_s, x_r, c_s, c_r,
):
    pairs = ((k_hbm, k_ref), (v_hbm, v_ref), (q_hbm, q_ref), (g_hbm, g_ref))
    loads = [pltpu.make_async_copy(*pair, in_s.at[n]) for n, pair in enumerate(pairs)]
    for load in loads:
        load.start()
    seg, lane, other, across = places()
    heads_here = qd.shape[1]
    barrier = greet(lanes)

    def pack(left, right, to):
        for h in range(lanes * heads_here):
            columns = slice(h * HDIM, (h + 1) * HDIM)
            to[h // heads_here, h % heads_here] = join(left[:, columns], right[:, columns])

    loads[0].wait()
    loads[1].wait()
    pack(k_ref, v_ref, kv_out)
    pl.semaphore_wait(barrier, lanes + 1)

    def kv_copy(i, target, source):
        return remote(kv_out.at[target], kv.at[seg, source], kv_s.at[i], kv_r.at[i], (seg, target))

    def qd_copy(i, target, source):
        return remote(qd_out.at[target], qd.at[source], qd_s.at[i], qd_r.at[i], (seg, target))

    def x_copy(i, source, whose):
        return remote(kv.at[whose, source], kv.at[whose, source], x_s.at[i], x_r.at[i], (across, lane))

    def c_copy(n, i, source, whose):
        block = kv.at[whose, source]
        return remote(block, block, c_s.at[n, i], c_r.at[n, i], (other, lane))

    def ahead(i):
        return lax.rem(lane + i, lanes)

    def behind(i):
        return lax.rem(lane + lanes - i, lanes)

    loop(1, lanes, lambda i: kv_copy(i, ahead(i), lane).start())
    kv[seg, lane] = kv_out[lane]
    x_copy(0, lane, seg).start()
    c_copy(0, 0, lane, seg).start()
    loads[2].wait()
    loads[3].wait()
    pack(q_ref, g_ref, qd_out)
    qd[lane] = qd_out[lane]

    def relay(i):
        x_copy(i, behind(i), across).wait_recv()
        c_copy(1, i, behind(i), across).start()

    def arrive(i):
        kv_copy(i, lane, behind(i)).wait_recv()
        x_copy(i, behind(i), seg).start()
        qd_copy(i, ahead(i), lane).start()
        c_copy(0, i, behind(i), seg).start()
        relay(i - 1)

    loop(1, lanes, arrive)
    relay(lanes - 1)

    def finish(i):
        c_copy(0, i, behind(i), other).wait_recv()
        c_copy(1, i, behind(i), lax.rem(other + 2, 4)).wait_recv()
        x_copy(i, behind(i), seg).wait_send()
        c_copy(0, i, behind(i), seg).wait_send()
        c_copy(1, i, behind(i), across).wait_send()

    loop(0, lanes, finish)

    def finish_lanes(i):
        qd_copy(i, lane, behind(i)).wait_recv()
        qd_copy(i, ahead(i), lane).wait_send()
        kv_copy(i, ahead(i), lane).wait_send()

    loop(1, lanes, finish_lanes)


def return_kernel(
    lanes, od, dkv, od_in, end_in, core_in, x_out, x_in, end_out,
    od_s, od_r, c_s, c_r, x_s, x_r, e_s, e_r,
):
    seg, lane, other, across = places()
    heads_here = od.shape[1]
    barrier = greet(lanes)

    def ahead(i):
        return lax.rem(lane + i, lanes)

    def behind(i):
        return lax.rem(lane + lanes - i, lanes)

    def od_copy(i, target, source):
        return remote(od.at[target], od_in.at[source], od_s.at[i], od_r.at[i], (seg, target))

    def end_copy(i, target, source):
        return remote(end_out.at[target], end_in.at[source], e_s.at[i], e_r.at[i], (seg, target))

    def c_copy(n, i, whose):
        return remote(dkv.at[whose, ahead(i)], core_in.at[n, ahead(i)], c_s.at[n, i], c_r.at[n, i], (other, lane))

    def x_copy(i):
        return remote(x_out.at[ahead(i)], x_in.at[ahead(i)], x_s.at[i], x_r.at[i], (across, lane))

    def send(i):
        c_copy(1, i, lax.rem(other + 2, 4)).start()
        c_copy(0, i, other).start()

    def wide(block):
        return block.astype(jnp.float32)

    def reduce_core(i):
        c_copy(1, i, other).wait_recv()
        to = ahead(i)
        x_out[to] = (wide(dkv[across, to]) + wide(core_in[1, to])).astype(jnp.bfloat16)
        x_copy(i).start()

    def total(i):
        c_copy(0, i, other).wait_recv()
        x_copy(i).wait_recv()
        to = ahead(i)
        return (wide(dkv[seg, to]) + wide(core_in[0, to]) + wide(x_in[to])).astype(jnp.bfloat16)

    def reduce_chip(i):
        end_out[ahead(i)] = total(i)
        end_copy(i, ahead(i), lane).start()

    lag = min(2, lanes - 1)
    pl.semaphore_wait(barrier, lanes + 1)
    loop(1, lanes + 1, send)
    loop(1, lanes, lambda i: od_copy(i, ahead(i), lane).start())
    od_in[lane] = od[lane]
    loop(1, lag + 1, reduce_core)

    def both(i):
        reduce_core(i)
        reduce_chip(i - lag)

    loop(lag + 1, lanes + 1, both)
    loop(lanes + 1 - lag, lanes, reduce_chip)
    end_in[lane] = total(lanes)

    def finish(i):
        c_copy(0, i, other).wait_send()
        c_copy(1, i, other).wait_send()
        x_copy(i).wait_send()

    loop(1, lanes + 1, finish)

    def finish_lanes(i):
        od_copy(i, lane, behind(i)).wait_recv()
        end_copy(i, lane, behind(i)).wait_recv()
        od_copy(i, ahead(i), lane).wait_send()
        end_copy(i, ahead(i), lane).wait_send()

    loop(1, lanes, finish_lanes)


def unpack_kernel(od, dkv, out_ref, dq_ref, dk_ref, dv_ref):
    for block, left, right in ((od, dq_ref, out_ref), (dkv, dk_ref, dv_ref)):
        heads_here = block.shape[1]
        for h in range(0, block.shape[0] * heads_here, 2):
            a, b = (block[g // heads_here, g % heads_here] for g in (h, h + 1))
            columns = slice(h * HDIM, (h + 2) * HDIM)
            left[:, columns] = join(a[:, :HDIM], b[:, :HDIM])
            right[:, columns] = join(a[:, HDIM:], b[:, HDIM:])


def comm_params(number, chunks, block):
    chunk_bytes = 2 * math.prod(block)
    return pltpu.CompilerParams(
        collective_id=number, has_side_effects=True, vmem_limit_bytes=4 * MIB + chunks * chunk_bytes
    )


def on_device(lanes, query_rows, key_rows, value_rows, out_grad, block_lists, block_counts):
    rows, width = query_rows.shape
    heads_here = width // HDIM // lanes
    segs = 4
    block = (heads_here, rows, PAIR)
    vmem = pl.BlockSpec(memory_space=pltpu.VMEM)
    dma = pltpu.SemaphoreType.DMA
    half = jnp.bfloat16
    chunks = jax.ShapeDtypeStruct((lanes, *block), half)

    qd, kv = pl.pallas_call(
        functools.partial(gather_kernel, lanes),
        out_shape=(chunks, jax.ShapeDtypeStruct((segs, lanes, *block), half)),
        in_specs=[pl.BlockSpec(memory_space=pltpu.HBM)] * 4,
        out_specs=(vmem, vmem),
        scratch_shapes=[pltpu.VMEM((rows, width), half)] * 4
        + [pltpu.VMEM((lanes, *block), half)] * 2
        + [dma((4,))]
        + [dma((lanes,))] * 6
        + [dma((2, lanes))] * 2,
        compiler_params=comm_params(0, 10 * lanes, block),
        name="gather",
    )(*(pltpu.with_memory_space_constraint(a, pltpu.HBM) for a in (query_rows, key_rows, value_rows, out_grad)))

    qd = qd.transpose(1, 0, 2, 3).reshape(heads_here, lanes * rows, PAIR)
    kv = kv.transpose(2, 0, 1, 3, 4).reshape(heads_here, segs * lanes * rows, PAIR)
    od, dkv = attention(block_lists, block_counts, qd, kv)
    od = od.reshape(heads_here, lanes, rows, PAIR).transpose(1, 0, 2, 3)
    dkv = dkv.reshape(heads_here, segs, lanes, rows, PAIR).transpose(1, 2, 0, 3, 4)

    od, dkv = pl.pallas_call(
        functools.partial(return_kernel, lanes),
        out_shape=[chunks] * 2,
        in_specs=[vmem] * 2,
        out_specs=[vmem] * 2,
        scratch_shapes=[pltpu.VMEM((2, lanes, *block), half)]
        + [pltpu.VMEM((lanes, *block), half)] * 3
        + [dma((lanes + 1,))] * 2
        + [dma((2, lanes + 1))] * 2
        + [dma((lanes + 1,))] * 4,
        compiler_params=comm_params(1, 14 * lanes, block),
        name="scatter",
    )(od, dkv)

    return pl.pallas_call(
        unpack_kernel,
        out_shape=[jax.ShapeDtypeStruct((rows, width), half)] * 4,
        in_specs=[vmem] * 2,
        out_specs=[vmem] * 4,
        compiler_params=pltpu.CompilerParams(vmem_limit_bytes=4 * MIB + 32 * rows * width),
        name="unpack",
    )(od, dkv)


def solution(mesh):
    tokens = P(("blk", "uly"), None)
    return jax.shard_map(
        functools.partial(on_device, mesh.shape["uly"]),
        mesh=mesh,
        in_specs=(tokens, tokens, tokens, tokens, P("blk", None), P("blk")),
        out_specs=(tokens, tokens, tokens, tokens),
        check_vma=False,
    )
```

```python
import functools
import math

import jax
import jax.numpy as jnp
from jax import lax
from jax.experimental import pallas as pl
from jax.experimental.pallas import tpu as pltpu
from jax.sharding import PartitionSpec as P

HDIM = 64
BLK = 64
KSEL = 8
PAIR = 2 * HDIM
SCALE = 1.0 / math.sqrt(HDIM)
GROUP = 16
MIB = 1024 * 1024


def dot(a, b, dims):
    return lax.dot_general(a, b, (dims, ((), ())), preferred_element_type=jnp.float32)


def attention_kernel(group, lists_hbm, counts_hbm, qd, kv, od, dkv, lists, counts, acc, sems):
    loads = (
        pltpu.make_async_copy(lists_hbm, lists, sems.at[0]),
        pltpu.make_async_copy(counts_hbm, counts, sems.at[1]),
    )
    for load in loads:
        load.start()
    for h in range(qd.shape[0]):
        acc[...] = jnp.zeros_like(acc)
        if h == 0:
            for load in loads:
                load.wait()
        attend_head(group, lists, counts, qd.at[h], kv.at[h], od.at[h], acc)
        dkv[h] = acc[...].astype(dkv.dtype)


def attend_head(group, lists, counts, qd_ref, kv_ref, od_ref, acc):
    local_blocks = qd_ref.shape[0] // BLK
    lane = lax.broadcasted_iota(jnp.int32, (BLK, PAIR), 1)
    first = lane < HDIM
    column = lax.broadcasted_iota(jnp.int32, (BLK, KSEL * BLK), 1)

    def one_block(b):
        rows = pl.ds(pl.multiple_of(b * BLK, BLK), BLK)
        picks = [pl.ds(pl.multiple_of(lists[j, b] * BLK, BLK), BLK) for j in range(KSEL)]
        qd = qd_ref[rows, :]
        zero = jnp.zeros_like(qd)
        diag = jnp.concatenate([jnp.where(first, qd * SCALE, zero), jnp.where(first, zero, qd)], axis=0)
        kv = jnp.concatenate([kv_ref[pick, :] for pick in picks], axis=0)
        both = dot(diag, kv, ((1,), (1,)))
        scores = jnp.where(column < counts[b] * BLK, both[:BLK], -1e30)
        weights = jnp.exp(scores - jnp.max(scores, axis=1, keepdims=True))
        prob = weights * (1.0 / jnp.sum(weights, axis=1, keepdims=True))
        rounded = prob.astype(jnp.bfloat16)
        delta = jnp.sum(rounded.astype(jnp.float32) * both[BLK:], axis=1, keepdims=True)
        grad_score = (prob * (both[BLK:] - delta)).astype(jnp.bfloat16)
        stacked = jnp.concatenate([grad_score, rounded], axis=0)
        rows_out = dot(stacked, kv, ((1,), (0,)))
        od_ref[rows, :] = jnp.where(first, rows_out[:BLK] * SCALE, rows_out[BLK:]).astype(jnp.bfloat16)
        terms = dot(stacked, diag, ((0,), (0,)))
        return picks, terms

    def turn(g, carry):
        done = [one_block(g * group + i) for i in range(group)]
        for picks, terms in done:
            for j, pick in enumerate(picks):
                acc[pick, :] += terms[j * BLK : (j + 1) * BLK]
        return carry

    lax.fori_loop(0, local_blocks // group, turn, 0)

def attention(block_lists, block_counts, qd, kv):
    heads_here, seg_rows, _ = qd.shape
    all_rows = kv.shape[1]
    vmem = pl.BlockSpec(memory_space=pltpu.VMEM)
    hbm = pl.BlockSpec(memory_space=pltpu.HBM)
    lists = block_lists.T
    limit = 6 * MIB + 4 * all_rows * PAIR + 4 * heads_here * (all_rows + seg_rows) * PAIR
    return pl.pallas_call(
        functools.partial(attention_kernel, math.gcd(GROUP, seg_rows // BLK)),
        out_shape=(
            jax.ShapeDtypeStruct(qd.shape, jnp.bfloat16),
            jax.ShapeDtypeStruct(kv.shape, jnp.bfloat16),
        ),
        in_specs=[hbm, hbm, vmem, vmem],
        out_specs=(vmem, vmem),
        scratch_shapes=[
            pltpu.SMEM(lists.shape, jnp.int32),
            pltpu.SMEM(block_counts.shape, jnp.int32),
            pltpu.VMEM((all_rows, PAIR), jnp.float32),
            pltpu.SemaphoreType.DMA((2,)),
        ],
        compiler_params=pltpu.CompilerParams(vmem_limit_bytes=limit),
        name="attention",
    )(
        pltpu.with_memory_space_constraint(lists, pltpu.HBM),
        pltpu.with_memory_space_constraint(block_counts, pltpu.HBM),
        qd,
        kv,
    )


MESH = pl.DeviceIdType.MESH


def places():
    seg, lane = lax.axis_index("blk"), lax.axis_index("uly")
    core = lax.rem(seg, 2)
    return seg, lane, seg + 1 - 2 * core, lax.rem(seg + 2, 4)


def remote(src, dst, send, recv, device):
    return pltpu.make_async_remote_copy(
        src_ref=src, dst_ref=dst, send_sem=send, recv_sem=recv, device_id=device, device_id_type=MESH
    )


def greet(lanes, diagonal=False):
    seg, lane, other, across = places()
    barrier = pltpu.get_barrier_semaphore()

    def one(i, carry):
        device = (seg, lax.rem(lane + i, lanes))
        pl.semaphore_signal(barrier, inc=1, device_id=device, device_id_type=MESH)
        return carry

    lax.fori_loop(1, lanes, one, 0)
    for near in (other, across, lax.rem(other + 2, 4))[: 3 if diagonal else 2]:
        pl.semaphore_signal(barrier, inc=1, device_id=(near, lane), device_id_type=MESH)
    return barrier


def loop(start, stop, body):
    lax.fori_loop(start, stop, lambda i, carry: (body(i), carry)[1], 0)


def join(left, right):
    return jnp.concatenate([left, right], axis=1)


def gather_kernel(
    lanes, q_hbm, k_hbm, v_hbm, g_hbm, qd, kv,
    k_ref, v_ref, q_ref, g_ref, qd_out, kv_out, in_s, qd_s, qd_r, kv_s, kv_r, x_s, x_r, c_s, c_r,
):
    pairs = ((k_hbm, k_ref), (v_hbm, v_ref), (q_hbm, q_ref), (g_hbm, g_ref))
    loads = [pltpu.make_async_copy(*pair, in_s.at[n]) for n, pair in enumerate(pairs)]
    for load in loads:
        load.start()
    seg, lane, other, across = places()
    heads_here = qd.shape[1]
    barrier = greet(lanes, True)

    def pack(left, right, to):
        for h in range(lanes * heads_here):
            columns = slice(h * HDIM, (h + 1) * HDIM)
            to[h // heads_here, h % heads_here] = join(left[:, columns], right[:, columns])

    loads[0].wait()
    loads[1].wait()
    pack(k_ref, v_ref, kv_out)
    pl.semaphore_wait(barrier, lanes + 2)

    def kv_copy(i, target, source):
        return remote(kv_out.at[target], kv.at[seg, source], kv_s.at[i], kv_r.at[i], (seg, target))

    def qd_copy(i, target, source):
        return remote(qd_out.at[target], qd.at[source], qd_s.at[i], qd_r.at[i], (seg, target))

    def x_copy(i, source, whose):
        return remote(kv.at[whose, source], kv.at[whose, source], x_s.at[i], x_r.at[i], (across, lane))

    def c_copy(n, i, source, whose):
        block = kv.at[whose, source]
        near = other if n == 0 else lax.rem(other + 2, 4)
        return remote(block, block, c_s.at[n, i], c_r.at[n, i], (near, lane))

    def ahead(i):
        return lax.rem(lane + i, lanes)

    def behind(i):
        return lax.rem(lane + lanes - i, lanes)

    loop(1, lanes, lambda i: kv_copy(i, ahead(i), lane).start())
    kv[seg, lane] = kv_out[lane]
    x_copy(0, lane, seg).start()
    c_copy(1, 0, lane, seg).start()
    c_copy(0, 0, lane, seg).start()
    loads[2].wait()
    loads[3].wait()
    pack(q_ref, g_ref, qd_out)
    qd[lane] = qd_out[lane]

    def arrive(i):
        kv_copy(i, lane, behind(i)).wait_recv()
        x_copy(i, behind(i), seg).start()
        qd_copy(i, ahead(i), lane).start()
        c_copy(1, i, behind(i), seg).start()
        c_copy(0, i, behind(i), seg).start()

    loop(1, lanes, arrive)
    loop(0, lanes, lambda i: x_copy(i, behind(i), across).wait_recv())

    def finish(i):
        c_copy(0, i, behind(i), other).wait_recv()
        c_copy(1, i, behind(i), lax.rem(other + 2, 4)).wait_recv()
        x_copy(i, behind(i), seg).wait_send()
        c_copy(0, i, behind(i), seg).wait_send()
        c_copy(1, i, behind(i), seg).wait_send()

    loop(0, lanes, finish)

    def finish_lanes(i):
        qd_copy(i, lane, behind(i)).wait_recv()
        qd_copy(i, ahead(i), lane).wait_send()
        kv_copy(i, ahead(i), lane).wait_send()

    loop(1, lanes, finish_lanes)


def return_kernel(
    lanes, od, dkv, od_in, end_in, core_in, x_out, x_in, end_out,
    od_s, od_r, c_s, c_r, x_s, x_r, e_s, e_r,
):
    seg, lane, other, across = places()
    heads_here = od.shape[1]
    barrier = greet(lanes)

    def ahead(i):
        return lax.rem(lane + i, lanes)

    def behind(i):
        return lax.rem(lane + lanes - i, lanes)

    def od_copy(i, target, source):
        return remote(od.at[target], od_in.at[source], od_s.at[i], od_r.at[i], (seg, target))

    def end_copy(i, target, source):
        return remote(end_out.at[target], end_in.at[source], e_s.at[i], e_r.at[i], (seg, target))

    def c_copy(n, i, whose):
        return remote(dkv.at[whose, ahead(i)], core_in.at[n, ahead(i)], c_s.at[n, i], c_r.at[n, i], (other, lane))

    def x_copy(i):
        return remote(x_out.at[ahead(i)], x_in.at[ahead(i)], x_s.at[i], x_r.at[i], (across, lane))

    def send(i):
        c_copy(1, i, lax.rem(other + 2, 4)).start()
        c_copy(0, i, other).start()

    def wide(block):
        return block.astype(jnp.float32)

    def reduce_core(i):
        c_copy(1, i, other).wait_recv()
        to = ahead(i)
        x_out[to] = (wide(dkv[across, to]) + wide(core_in[1, to])).astype(jnp.bfloat16)
        x_copy(i).start()

    def total(i):
        c_copy(0, i, other).wait_recv()
        x_copy(i).wait_recv()
        to = ahead(i)
        return (wide(dkv[seg, to]) + wide(core_in[0, to]) + wide(x_in[to])).astype(jnp.bfloat16)

    def reduce_chip(i):
        end_out[ahead(i)] = total(i)
        end_copy(i, ahead(i), lane).start()

    lag = min(2, lanes - 1)
    pl.semaphore_wait(barrier, lanes + 1)
    loop(1, lanes + 1, send)
    loop(1, lanes, lambda i: od_copy(i, ahead(i), lane).start())
    od_in[lane] = od[lane]
    loop(1, lag + 1, reduce_core)

    def both(i):
        reduce_core(i)
        reduce_chip(i - lag)

    loop(lag + 1, lanes + 1, both)
    loop(lanes + 1 - lag, lanes, reduce_chip)
    end_in[lane] = total(lanes)

    def finish(i):
        c_copy(0, i, other).wait_send()
        c_copy(1, i, other).wait_send()
        x_copy(i).wait_send()

    loop(1, lanes + 1, finish)

    def finish_lanes(i):
        od_copy(i, lane, behind(i)).wait_recv()
        end_copy(i, lane, behind(i)).wait_recv()
        od_copy(i, ahead(i), lane).wait_send()
        end_copy(i, ahead(i), lane).wait_send()

    loop(1, lanes, finish_lanes)


def unpack_kernel(od, dkv, out_ref, dq_ref, dk_ref, dv_ref):
    for block, left, right in ((od, dq_ref, out_ref), (dkv, dk_ref, dv_ref)):
        heads_here = block.shape[1]
        for h in range(0, block.shape[0] * heads_here, 2):
            a, b = (block[g // heads_here, g % heads_here] for g in (h, h + 1))
            columns = slice(h * HDIM, (h + 2) * HDIM)
            left[:, columns] = join(a[:, :HDIM], b[:, :HDIM])
            right[:, columns] = join(a[:, HDIM:], b[:, HDIM:])


def comm_params(number, chunks, block):
    chunk_bytes = 2 * math.prod(block)
    return pltpu.CompilerParams(
        collective_id=number, has_side_effects=True, vmem_limit_bytes=4 * MIB + chunks * chunk_bytes
    )


def on_device(lanes, query_rows, key_rows, value_rows, out_grad, block_lists, block_counts):
    rows, width = query_rows.shape
    heads_here = width // HDIM // lanes
    segs = 4
    block = (heads_here, rows, PAIR)
    vmem = pl.BlockSpec(memory_space=pltpu.VMEM)
    dma = pltpu.SemaphoreType.DMA
    half = jnp.bfloat16
    chunks = jax.ShapeDtypeStruct((lanes, *block), half)

    qd, kv = pl.pallas_call(
        functools.partial(gather_kernel, lanes),
        out_shape=(chunks, jax.ShapeDtypeStruct((segs, lanes, *block), half)),
        in_specs=[pl.BlockSpec(memory_space=pltpu.HBM)] * 4,
        out_specs=(vmem, vmem),
        scratch_shapes=[pltpu.VMEM((rows, width), half)] * 4
        + [pltpu.VMEM((lanes, *block), half)] * 2
        + [dma((4,))]
        + [dma((lanes,))] * 6
        + [dma((2, lanes))] * 2,
        compiler_params=comm_params(0, 10 * lanes, block),
        name="gather",
    )(*(pltpu.with_memory_space_constraint(a, pltpu.HBM) for a in (query_rows, key_rows, value_rows, out_grad)))

    qd = qd.transpose(1, 0, 2, 3).reshape(heads_here, lanes * rows, PAIR)
    kv = kv.transpose(2, 0, 1, 3, 4).reshape(heads_here, segs * lanes * rows, PAIR)
    od, dkv = attention(block_lists, block_counts, qd, kv)
    od = od.reshape(heads_here, lanes, rows, PAIR).transpose(1, 0, 2, 3)
    dkv = dkv.reshape(heads_here, segs, lanes, rows, PAIR).transpose(1, 2, 0, 3, 4)

    od, dkv = pl.pallas_call(
        functools.partial(return_kernel, lanes),
        out_shape=[chunks] * 2,
        in_specs=[vmem] * 2,
        out_specs=[vmem] * 2,
        scratch_shapes=[pltpu.VMEM((2, lanes, *block), half)]
        + [pltpu.VMEM((lanes, *block), half)] * 3
        + [dma((lanes + 1,))] * 2
        + [dma((2, lanes + 1))] * 2
        + [dma((lanes + 1,))] * 4,
        compiler_params=comm_params(1, 14 * lanes, block),
        name="scatter",
    )(od, dkv)

    return pl.pallas_call(
        unpack_kernel,
        out_shape=[jax.ShapeDtypeStruct((rows, width), half)] * 4,
        in_specs=[vmem] * 2,
        out_specs=[vmem] * 4,
        compiler_params=pltpu.CompilerParams(vmem_limit_bytes=4 * MIB + 32 * rows * width),
        name="unpack",
    )(od, dkv)


def solution(mesh):
    tokens = P(("blk", "uly"), None)
    return jax.shard_map(
        functools.partial(on_device, mesh.shape["uly"]),
        mesh=mesh,
        in_specs=(tokens, tokens, tokens, tokens, P("blk", None), P("blk")),
        out_specs=(tokens, tokens, tokens, tokens),
        check_vma=False,
    )
```

```python
import functools
import math

import jax
import jax.numpy as jnp
from jax import lax
from jax.experimental import pallas as pl
from jax.experimental.pallas import tpu as pltpu
from jax.sharding import PartitionSpec as P

HDIM = 64
BLK = 64
KSEL = 8
PAIR = 2 * HDIM
SCALE = 1.0 / math.sqrt(HDIM)
GROUP = 16
MIB = 1024 * 1024


def dot(a, b, dims):
    return lax.dot_general(a, b, (dims, ((), ())), preferred_element_type=jnp.float32)


def attention_kernel(group, lists_hbm, counts_hbm, qd, kv, od, dkv, lists, counts, acc, sems):
    loads = (
        pltpu.make_async_copy(lists_hbm, lists, sems.at[0]),
        pltpu.make_async_copy(counts_hbm, counts, sems.at[1]),
    )
    for load in loads:
        load.start()
    for h in range(qd.shape[0]):
        acc[...] = jnp.zeros_like(acc)
        if h == 0:
            for load in loads:
                load.wait()
        attend_head(group, lists, counts, qd.at[h], kv.at[h], od.at[h], acc)
        dkv[h] = acc[...].astype(dkv.dtype)


def attend_head(group, lists, counts, qd_ref, kv_ref, od_ref, acc):
    local_blocks = qd_ref.shape[0] // BLK
    lane = lax.broadcasted_iota(jnp.int32, (BLK, PAIR), 1)
    first = lane < HDIM
    column = lax.broadcasted_iota(jnp.int32, (BLK, KSEL * BLK), 1)

    def one_block(b):
        rows = pl.ds(pl.multiple_of(b * BLK, BLK), BLK)
        picks = [pl.ds(pl.multiple_of(lists[j, b] * BLK, BLK), BLK) for j in range(KSEL)]
        qd = qd_ref[rows, :]
        zero = jnp.zeros_like(qd)
        diag = jnp.concatenate([jnp.where(first, qd * SCALE, zero), jnp.where(first, zero, qd)], axis=0)
        kv = jnp.concatenate([kv_ref[pick, :] for pick in picks], axis=0)
        both = dot(diag, kv, ((1,), (1,)))
        scores = jnp.where(column < counts[b] * BLK, both[:BLK], -1e30)
        weights = jnp.exp(scores - jnp.max(scores, axis=1, keepdims=True))
        prob = weights * (1.0 / jnp.sum(weights, axis=1, keepdims=True))
        rounded = prob.astype(jnp.bfloat16)
        delta = jnp.sum(rounded.astype(jnp.float32) * both[BLK:], axis=1, keepdims=True)
        grad_score = (prob * (both[BLK:] - delta)).astype(jnp.bfloat16)
        stacked = jnp.concatenate([grad_score, rounded], axis=0)
        rows_out = dot(stacked, kv, ((1,), (0,)))
        od_ref[rows, :] = jnp.where(first, rows_out[:BLK] * SCALE, rows_out[BLK:]).astype(jnp.bfloat16)
        terms = dot(stacked, diag, ((0,), (0,)))
        return picks, terms

    def turn(g, carry):
        done = [one_block(g * group + i) for i in range(group)]
        for picks, terms in done:
            for j, pick in enumerate(picks):
                acc[pick, :] += terms[j * BLK : (j + 1) * BLK]
        return carry

    lax.fori_loop(0, local_blocks // group, turn, 0)

def attention(block_lists, block_counts, qd, kv):
    heads_here, seg_rows, _ = qd.shape
    all_rows = kv.shape[1]
    vmem = pl.BlockSpec(memory_space=pltpu.VMEM)
    hbm = pl.BlockSpec(memory_space=pltpu.HBM)
    lists = block_lists.T
    limit = 6 * MIB + 4 * all_rows * PAIR + 4 * heads_here * (all_rows + seg_rows) * PAIR
    return pl.pallas_call(
        functools.partial(attention_kernel, math.gcd(GROUP, seg_rows // BLK)),
        out_shape=(
            jax.ShapeDtypeStruct(qd.shape, jnp.bfloat16),
            jax.ShapeDtypeStruct(kv.shape, jnp.bfloat16),
        ),
        in_specs=[hbm, hbm, vmem, vmem],
        out_specs=(vmem, vmem),
        scratch_shapes=[
            pltpu.SMEM(lists.shape, jnp.int32),
            pltpu.SMEM(block_counts.shape, jnp.int32),
            pltpu.VMEM((all_rows, PAIR), jnp.float32),
            pltpu.SemaphoreType.DMA((2,)),
        ],
        compiler_params=pltpu.CompilerParams(vmem_limit_bytes=limit),
        name="attention",
    )(
        pltpu.with_memory_space_constraint(lists, pltpu.HBM),
        pltpu.with_memory_space_constraint(block_counts, pltpu.HBM),
        qd,
        kv,
    )


MESH = pl.DeviceIdType.MESH


def places():
    seg, lane = lax.axis_index("blk"), lax.axis_index("uly")
    core = lax.rem(seg, 2)
    return seg, lane, seg + 1 - 2 * core, lax.rem(seg + 2, 4)


def remote(src, dst, send, recv, device):
    return pltpu.make_async_remote_copy(
        src_ref=src, dst_ref=dst, send_sem=send, recv_sem=recv, device_id=device, device_id_type=MESH
    )


def greet(lanes, diagonal=False):
    seg, lane, other, across = places()
    barrier = pltpu.get_barrier_semaphore()

    def one(i, carry):
        device = (seg, lax.rem(lane + i, lanes))
        pl.semaphore_signal(barrier, inc=1, device_id=device, device_id_type=MESH)
        return carry

    lax.fori_loop(1, lanes, one, 0)
    for near in (other, across, lax.rem(other + 2, 4))[: 3 if diagonal else 2]:
        pl.semaphore_signal(barrier, inc=1, device_id=(near, lane), device_id_type=MESH)
    return barrier


def loop(start, stop, body):
    lax.fori_loop(start, stop, lambda i, carry: (body(i), carry)[1], 0)


def join(left, right):
    return jnp.concatenate([left, right], axis=1)


def gather_kernel(
    lanes, q_hbm, k_hbm, v_hbm, g_hbm, qd, kv,
    k_ref, v_ref, q_ref, g_ref, qd_out, kv_out, in_s, qd_s, qd_r, kv_s, kv_r, x_s, x_r, c_s, c_r,
):
    pairs = ((k_hbm, k_ref), (v_hbm, v_ref), (q_hbm, q_ref), (g_hbm, g_ref))
    loads = [pltpu.make_async_copy(*pair, in_s.at[n]) for n, pair in enumerate(pairs)]
    for load in loads:
        load.start()
    seg, lane, other, across = places()
    heads_here = qd.shape[1]
    barrier = greet(lanes, True)

    def pack(left, right, to):
        for h in range(lanes * heads_here):
            columns = slice(h * HDIM, (h + 1) * HDIM)
            to[h // heads_here, h % heads_here] = join(left[:, columns], right[:, columns])

    loads[0].wait()
    loads[1].wait()
    pack(k_ref, v_ref, kv_out)
    pl.semaphore_wait(barrier, lanes + 2)

    def kv_copy(i, target, source):
        return remote(kv_out.at[target], kv.at[seg, source], kv_s.at[i], kv_r.at[i], (seg, target))

    def qd_copy(i, target, source):
        return remote(qd_out.at[target], qd.at[source], qd_s.at[i], qd_r.at[i], (seg, target))

    def x_copy(i, source, whose):
        return remote(kv.at[whose, source], kv.at[whose, source], x_s.at[i], x_r.at[i], (across, lane))

    def c_copy(n, i, source, whose):
        block = kv.at[whose, source]
        near = other if n == 0 else lax.rem(other + 2, 4)
        return remote(block, block, c_s.at[n, i], c_r.at[n, i], (near, lane))

    def ahead(i):
        return lax.rem(lane + i, lanes)

    def behind(i):
        return lax.rem(lane + lanes - i, lanes)

    loop(1, lanes, lambda i: kv_copy(i, ahead(i), lane).start())
    kv[seg, lane] = kv_out[lane]
    x_copy(0, lane, seg).start()
    c_copy(1, 0, lane, seg).start()
    c_copy(0, 0, lane, seg).start()
    loads[2].wait()
    loads[3].wait()
    pack(q_ref, g_ref, qd_out)
    qd[lane] = qd_out[lane]

    def arrive(i):
        kv_copy(i, lane, behind(i)).wait_recv()
        x_copy(i, behind(i), seg).start()
        qd_copy(i, ahead(i), lane).start()
        c_copy(1, i, behind(i), seg).start()
        c_copy(0, i, behind(i), seg).start()

    loop(1, lanes, arrive)
    loop(0, lanes, lambda i: x_copy(i, behind(i), across).wait_recv())

    def finish(i):
        c_copy(0, i, behind(i), other).wait_recv()
        c_copy(1, i, behind(i), lax.rem(other + 2, 4)).wait_recv()
        x_copy(i, behind(i), seg).wait_send()
        c_copy(0, i, behind(i), seg).wait_send()
        c_copy(1, i, behind(i), seg).wait_send()

    loop(0, lanes, finish)

    def finish_lanes(i):
        qd_copy(i, lane, behind(i)).wait_recv()
        qd_copy(i, ahead(i), lane).wait_send()
        kv_copy(i, ahead(i), lane).wait_send()

    loop(1, lanes, finish_lanes)


def return_kernel(
    lanes, od, dkv, od_in, end_in, core_in, x_out, x_in, end_out,
    od_s, od_r, c_s, c_r, x_s, x_r, e_s, e_r,
):
    seg, lane, other, across = places()
    heads_here = od.shape[1]
    barrier = greet(lanes)

    def ahead(i):
        return lax.rem(lane + i, lanes)

    def behind(i):
        return lax.rem(lane + lanes - i, lanes)

    def od_copy(i, target, source):
        return remote(od.at[target], od_in.at[source], od_s.at[i], od_r.at[i], (seg, target))

    def end_copy(i, target, source):
        return remote(end_out.at[target], end_in.at[source], e_s.at[i], e_r.at[i], (seg, target))

    def c_copy(n, i, whose):
        return remote(dkv.at[whose, ahead(i)], core_in.at[n, ahead(i)], c_s.at[n, i], c_r.at[n, i], (other, lane))

    def x_copy(i):
        return remote(x_out.at[ahead(i)], x_in.at[ahead(i)], x_s.at[i], x_r.at[i], (across, lane))

    def send(i):
        c_copy(1, i, lax.rem(other + 2, 4)).start()
        c_copy(0, i, other).start()

    def wide(block):
        return block.astype(jnp.float32)

    def reduce_core(i):
        c_copy(1, i, other).wait_recv()
        to = ahead(i)
        x_out[to] = (wide(dkv[across, to]) + wide(core_in[1, to])).astype(jnp.bfloat16)
        x_copy(i).start()

    def total(i):
        c_copy(0, i, other).wait_recv()
        x_copy(i).wait_recv()
        to = ahead(i)
        return (wide(dkv[seg, to]) + wide(core_in[0, to]) + wide(x_in[to])).astype(jnp.bfloat16)

    def reduce_chip(i):
        end_out[ahead(i)] = total(i)
        end_copy(i, ahead(i), lane).start()

    lag = min(4, lanes - 1)
    pl.semaphore_wait(barrier, lanes + 1)
    loop(1, lanes + 1, send)
    loop(1, lanes, lambda i: od_copy(i, ahead(i), lane).start())
    od_in[lane] = od[lane]
    loop(1, lag + 1, reduce_core)

    def both(i):
        reduce_core(i)
        reduce_chip(i - lag)

    loop(lag + 1, lanes + 1, both)
    loop(lanes + 1 - lag, lanes, reduce_chip)
    end_in[lane] = total(lanes)

    def finish(i):
        c_copy(0, i, other).wait_send()
        c_copy(1, i, other).wait_send()
        x_copy(i).wait_send()

    loop(1, lanes + 1, finish)

    def finish_lanes(i):
        od_copy(i, lane, behind(i)).wait_recv()
        end_copy(i, lane, behind(i)).wait_recv()
        od_copy(i, ahead(i), lane).wait_send()
        end_copy(i, ahead(i), lane).wait_send()

    loop(1, lanes, finish_lanes)


def unpack_kernel(od, dkv, out_ref, dq_ref, dk_ref, dv_ref):
    for block, left, right in ((od, dq_ref, out_ref), (dkv, dk_ref, dv_ref)):
        heads_here = block.shape[1]
        for h in range(0, block.shape[0] * heads_here, 2):
            a, b = (block[g // heads_here, g % heads_here] for g in (h, h + 1))
            columns = slice(h * HDIM, (h + 2) * HDIM)
            left[:, columns] = join(a[:, :HDIM], b[:, :HDIM])
            right[:, columns] = join(a[:, HDIM:], b[:, HDIM:])


def comm_params(number, chunks, block):
    chunk_bytes = 2 * math.prod(block)
    return pltpu.CompilerParams(
        collective_id=number, has_side_effects=True, vmem_limit_bytes=4 * MIB + chunks * chunk_bytes
    )


def on_device(lanes, query_rows, key_rows, value_rows, out_grad, block_lists, block_counts):
    rows, width = query_rows.shape
    heads_here = width // HDIM // lanes
    segs = 4
    block = (heads_here, rows, PAIR)
    vmem = pl.BlockSpec(memory_space=pltpu.VMEM)
    dma = pltpu.SemaphoreType.DMA
    half = jnp.bfloat16
    chunks = jax.ShapeDtypeStruct((lanes, *block), half)

    qd, kv = pl.pallas_call(
        functools.partial(gather_kernel, lanes),
        out_shape=(chunks, jax.ShapeDtypeStruct((segs, lanes, *block), half)),
        in_specs=[pl.BlockSpec(memory_space=pltpu.HBM)] * 4,
        out_specs=(vmem, vmem),
        scratch_shapes=[pltpu.VMEM((rows, width), half)] * 4
        + [pltpu.VMEM((lanes, *block), half)] * 2
        + [dma((4,))]
        + [dma((lanes,))] * 6
        + [dma((2, lanes))] * 2,
        compiler_params=comm_params(0, 10 * lanes, block),
        name="gather",
    )(*(pltpu.with_memory_space_constraint(a, pltpu.HBM) for a in (query_rows, key_rows, value_rows, out_grad)))

    qd = qd.transpose(1, 0, 2, 3).reshape(heads_here, lanes * rows, PAIR)
    kv = kv.transpose(2, 0, 1, 3, 4).reshape(heads_here, segs * lanes * rows, PAIR)
    od, dkv = attention(block_lists, block_counts, qd, kv)
    od = od.reshape(heads_here, lanes, rows, PAIR).transpose(1, 0, 2, 3)
    dkv = dkv.reshape(heads_here, segs, lanes, rows, PAIR).transpose(1, 2, 0, 3, 4)

    od, dkv = pl.pallas_call(
        functools.partial(return_kernel, lanes),
        out_shape=[chunks] * 2,
        in_specs=[vmem] * 2,
        out_specs=[vmem] * 2,
        scratch_shapes=[pltpu.VMEM((2, lanes, *block), half)]
        + [pltpu.VMEM((lanes, *block), half)] * 3
        + [dma((lanes + 1,))] * 2
        + [dma((2, lanes + 1))] * 2
        + [dma((lanes + 1,))] * 4,
        compiler_params=comm_params(1, 14 * lanes, block),
        name="scatter",
    )(od, dkv)

    return pl.pallas_call(
        unpack_kernel,
        out_shape=[jax.ShapeDtypeStruct((rows, width), half)] * 4,
        in_specs=[vmem] * 2,
        out_specs=[vmem] * 4,
        compiler_params=pltpu.CompilerParams(vmem_limit_bytes=4 * MIB + 32 * rows * width),
        name="unpack",
    )(od, dkv)


def solution(mesh):
    tokens = P(("blk", "uly"), None)
    return jax.shard_map(
        functools.partial(on_device, mesh.shape["uly"]),
        mesh=mesh,
        in_specs=(tokens, tokens, tokens, tokens, P("blk", None), P("blk")),
        out_specs=(tokens, tokens, tokens, tokens),
        check_vma=False,
    )
```
